512 devices in a mesh: prompt: 16 (over x, y_lo), feat: 32 (over y_hi, z, core).
Axes of the slice: x: 4, y: 8 (y_hi: 2, y_lo: 4; y = y_hi * 4 + y_lo), z: 8, core: 2. Of those that a mesh axis runs over, the one named last changes fastest.
Arguments:
- decoder: bfloat16 [8192, 5376], P('feat'), may hold values from -0.078125 to 0.078125
- encoder: bfloat16 [24576, 5376], P(('feat', 'prompt')), may hold values from -6 to 6
- row_ids: int32 [16, 512], P('prompt', 'feat'), may hold values from 0 to 255
- counts: int32 [16, 32], P('prompt'), may hold values from 1 to 16, 307 in all within a row
- activity: float32 [16, 512], P('prompt'), may hold values from 0.25 to 4
Outputs:
- edges: bfloat16 [16, 512, 24576], P('prompt', None, 'feat')
The draws below stay inside these ranges and needn't reach their ends.
Inputs may be any that keep to these rules, and one draw needn't show every extreme that they name: counts of one prompt sum to 307; some owner of each prompt holds exactly 16.
All inputs are finite; a program needn't handle non-finite values.
Results may differ from the reference program's by a relative error of at most 0.001.
Values may be sent and summed in bfloat16 or wider, within the bound.
No kernel may reach another device: no remote copies, remote signals or barrier semaphores. Data moves between devices by JAX's collectives and lax.ppermute only.
A program may use at most 64 MiB of HBM per device.

```python
import math
import jax
import jax.numpy as jnp
import numpy as np
from jax import lax

D = 5376
OWN_CAP = 16
SRC_DEV = 256
PROMPTS = 16
SLOTS = 512
FILLED = 307
FT = 24576
NSRC = 8192
N_FEAT = 32


def plant(values, key, least, top_value):
    longest = values.shape.index(max(values.shape))
    spots = []
    for shift in (0, 1):
        where = [jax.random.randint(jax.random.fold_in(key, axis), (), 0, length) for axis, length in enumerate(values.shape)]
        where[longest] = (where[longest] + shift) % values.shape[longest]
        spots.append(tuple(where))
    return values.at[spots[0]].set(least).at[spots[1]].set(top_value)


def block_scale(key, extent, split, smallest, top_value):
    level = 1.0
    for axis_at, shards_of in split:
        heights = jax.random.uniform(jax.random.fold_in(jax.random.fold_in(key, 6), axis_at), (shards_of,), jnp.float32, smallest / len(split), top_value / len(split))
        level = level * jnp.repeat(jnp.exp(heights), extent[axis_at] // shards_of).reshape((-1,) + (1,) * (len(extent) - 1 - axis_at))
    return level


def length_profile(count, total, bound, slope):
    loads = [(1 << 20) // math.isqrt(grade ** slope) + 1 for grade in range(2, count + 1)]
    spare, given = total - bound - (count - 1), [1] * (count - 1)
    while spare > 0:
        movable = [i for i in range(count - 1) if given[i] < bound]
        pool, remaining = sum([loads[i] for i in movable]), spare
        for i in movable:
            more = min(bound - given[i], max(1, remaining * loads[i] // pool), spare)
            given[i] = given[i] + more
            spare = spare - more
    return np.array([bound] + given)


def ragged(stream_key, count, total, bound, slope):
    if count == 2:
        one = jax.random.randint(stream_key, (), max(1, total - bound), min(bound, total - 1) + 1)
        return jnp.stack([one, total - one])
    tallies = jnp.asarray(length_profile(count, total, bound, slope), jnp.int32)
    twos = (count - 1) // 2
    donor, receiver = tallies[1:1 + 2 * twos:2], tallies[2:2 + 2 * twos:2]
    room = jnp.minimum(donor - 1, bound - receiver)
    moved = jax.random.randint(jax.random.fold_in(stream_key, 1), (twos,), 0, 1 << 20) % (room + 1)
    tallies = tallies.at[1:1 + 2 * twos:2].set(donor - moved).at[2:2 + 2 * twos:2].set(receiver + moved)
    return tallies[jax.random.permutation(jax.random.fold_in(stream_key, 2), count)]


def bell_draw(own_key, dims, spread, bound, cuts=(), held_as=jnp.bfloat16):
    values = jax.random.normal(own_key, dims, jnp.float32) * spread
    if len(cuts) > 0:
        values = block_scale(own_key, dims, cuts, -0.22, 0.18) * values
    return jnp.clip(values, min=-bound, max=bound).astype(held_as)


def setup_inputs(seed: int = 0) -> dict:
    key_of = jax.random.split(jax.random.key(seed), 6)
    decoder = bell_draw(key_of[0], (NSRC, D), D ** -0.5, 0.078125, ((0, 32),))
    encoder = bell_draw(key_of[1], (FT, D), 1.0, 6.0, ((0, 512),))
    row_ids = plant(jax.random.randint(key_of[2], (PROMPTS, SLOTS), 0, SRC_DEV), jax.random.fold_in(key_of[2], 1), 0, SRC_DEV - 1).astype(jnp.int32)
    counts = jax.vmap(lambda own: ragged(own, N_FEAT, FILLED, OWN_CAP, 2))(jax.random.split(key_of[3], PROMPTS)).reshape((PROMPTS, N_FEAT)).astype(jnp.int32)
    activity = jnp.clip(jnp.exp(math.log(4.0) - 2.7725887 * jax.random.uniform(key_of[4], (PROMPTS, SLOTS), jnp.float32) ** block_scale(key_of[4], (PROMPTS, SLOTS), ((0, 16),), -0.2, 0.2)), 0.25, 4.0)
    return {"decoder": decoder, "encoder": encoder, "row_ids": row_ids, "counts": counts, "activity": activity}


def reference(decoder, encoder, row_ids, counts, activity):
    owner_index = jnp.repeat(jnp.arange(N_FEAT, dtype=jnp.int32), OWN_CAP)
    slot_index = jnp.tile(jnp.arange(OWN_CAP, dtype=jnp.int32), N_FEAT)

    def per_prompt(inputs):
        local_ids, owner_counts, weights = inputs
        global_ids = (owner_index * SRC_DEV + local_ids).astype(jnp.int32)
        live_slots = slot_index < jnp.repeat(owner_counts, OWN_CAP)
        source_rows = jnp.where(live_slots[:, None], decoder[global_ids], jnp.zeros((), decoder.dtype))
        products = jnp.dot(source_rows, encoder.T, preferred_element_type=jnp.float32)
        return (weights[:, None] * products).astype(jnp.bfloat16)

    return lax.map(per_prompt, (row_ids, counts, activity))
```

```python
import jax
import jax.numpy as jnp
from jax import lax
from jax.experimental import pallas as pl
from jax.experimental.pallas import tpu as pltpu
from jax.sharding import PartitionSpec as P


AXES = ("prompt", "feat")


def routes(move):
    pairs = []
    for x in range(4):
        for y in range(8):
            for z in range(8):
                for core in range(2):
                    pairs.append((flat(x, y, z, core), flat(*move(x, y, z, core))))
    return pairs


def flat(x, y, z, core):
    prompt = (x % 4) * 4 + y % 4
    feat = ((y // 4) % 2 * 8 + z % 8) * 2 + core
    return prompt * 32 + feat


RING_X = routes(lambda x, y, z, c: (x + (1 - 2 * c), y, z, c))
RING_Y = routes(lambda x, y, z, c: (x, y // 4 * 4 + (y + (1 - 2 * c)) % 4, z, c))
RING_Z = routes(lambda x, y, z, c: (x, y, z + (1 - 2 * c), c))
OTHER_Y = routes(lambda x, y, z, c: (x, (y + 4) % 8, z, c))
CORE = routes(lambda x, y, z, c: (x, y, z, 1 - c))


def send(value, pairs):
    return lax.ppermute(value, AXES, pairs)


def product_kernel(row_at, act_ref, order_ref, *refs):
    n_rows = act_ref.shape[0]
    operands, (out_ref, rows, cols, acc, sem) = refs[:-5], refs[-5:]
    copies, at, into = [], 0, rows
    for i, operand in enumerate(operands):
        if at == n_rows and into is rows:
            at, into = 0, cols
        size = operand.shape[0]
        copies.append(pltpu.make_async_copy(operand, into.at[pl.ds(at, size)], sem.at[i]))
        at += size
    for copy in copies:
        copy.start()
    for copy in copies:
        copy.wait()
    depth = rows.shape[1]
    step = 768
    acc[...] = jnp.zeros_like(acc)

    @pl.loop(0, depth // step)
    def _(k):
        part = pl.ds(pl.multiple_of(k * step, step), step)
        acc[...] += lax.dot_general(
            rows[:, part], cols[:, part], (((1,), (1,)), ((), ())), preferred_element_type=jnp.float32
        )

    edges = (acc[...] * act_ref[...]).astype(jnp.bfloat16)
    placed = jnp.dot(edges, order_ref[...], preferred_element_type=jnp.float32).astype(jnp.bfloat16)
    for g in range(n_rows // 16):
        out_ref[pl.ds(pl.multiple_of(row_at[g], 16), 16), :] = placed[g * 16 : (g + 1) * 16]


def product(row_at, act, order, sources, targets):
    n_rows, n_cols, depth = act.shape[0], order.shape[0], sources[0].shape[1]
    whole = pl.BlockSpec(memory_space=pltpu.VMEM)
    return pl.pallas_call(
        product_kernel,
        out_shape=jax.ShapeDtypeStruct((n_rows, n_cols), jnp.bfloat16),
        in_specs=[pl.BlockSpec(memory_space=pltpu.SMEM), whole, whole]
        + [pl.BlockSpec(memory_space=pl.ANY)] * (len(sources) + len(targets)),
        out_specs=whole,
        scratch_shapes=[
            pltpu.VMEM((n_rows, depth), jnp.bfloat16),
            pltpu.VMEM((n_cols, depth), jnp.bfloat16),
            pltpu.VMEM((n_rows, n_cols), jnp.float32),
            pltpu.SemaphoreType.DMA((len(sources) + len(targets),)),
        ],
        compiler_params=pltpu.CompilerParams(vmem_limit_bytes=40 << 20),
        name="product",
    )(row_at, act, order, *sources, *targets)


def edges_of(decoder, encoder, row_ids, counts, activity):
    slot_count = row_ids.shape[1]
    prompt, owner = lax.axis_index("prompt"), lax.axis_index("feat")
    core, chip = owner % 2, owner // 2
    half, z = chip // 8, chip % 8
    x, y = prompt // 4, prompt % 4
    sign = 1 - 2 * core

    picked_rows = jnp.take(decoder, row_ids[0], axis=0)
    live_count = lax.dynamic_index_in_dim(counts[0], owner, 0, keepdims=False)
    live_slots = jnp.arange(slot_count, dtype=jnp.int32) < live_count
    source_rows = jnp.where(live_slots[:, None], picked_rows, jnp.zeros((), picked_rows.dtype))

    y0 = encoder
    y1 = send(y0, RING_Y)
    y2 = send(y1, RING_Y)
    y3 = send(y2, RING_Y)
    targets = []
    for block in (y0, y1, y2, y3):
        targets.append(block)
        for step in "123":
            block = send(block, RING_X)
            targets.append(block)

    both = jnp.concatenate([source_rows, send(source_rows, OTHER_Y)], axis=0)
    chunk = jnp.concatenate([both, send(both, CORE)], axis=0)
    sources, swaps = [chunk], []
    for step in "1234":
        chunk = send(chunk, RING_Z)
        sources.append(chunk)
        if step != "4":
            swaps.append(send(chunk, CORE))
    sources += swaps

    hop = jnp.array([0, -1, -2, -3, -4, 1, 2, 3], jnp.int32)[:, None, None]
    lead = jnp.array([0, 0, 0, 0, 0, 1, 1, 1], jnp.int32)[:, None, None]
    side = jnp.arange(2, dtype=jnp.int32)[None, :, None]
    flip = jnp.arange(2, dtype=jnp.int32)[None, None, :]
    z_from = (z + sign * hop) % 8
    feat_from = ((half ^ flip) * 8 + z_from) * 2 + (core ^ lead ^ side)
    group_from = feat_from.reshape(-1).astype(jnp.int32)
    ring = jnp.arange(4, dtype=jnp.int32)
    x_from = (x - sign * ring) % 4
    y_from = (y - sign * ring) % 4
    origin = (x_from[None, :] * 4 + y_from[:, None]).reshape(-1)
    width = encoder.shape[0]
    col_at = (origin[:, None] * width + jnp.arange(width, dtype=jnp.int32)[None, :]).reshape(-1)
    order = (col_at[:, None] == jnp.arange(col_at.shape[0], dtype=jnp.int32)[None, :]).astype(jnp.bfloat16)
    act = activity[0].reshape(-1, slot_count)[group_from].reshape(-1, 1)

    return product(group_from * slot_count, act, order, sources, targets)[None]


def solution(mesh):
    in_specs = (
        P("feat", None),
        P(("feat", "prompt"), None),
        P("prompt", "feat"),
        P("prompt", None),
        P("prompt", None),
    )
    out_specs = P("prompt", None, "feat")
    return jax.shard_map(edges_of, mesh=mesh, in_specs=in_specs, out_specs=out_specs, check_vma=False)
```

```python
import functools

import jax
import jax.numpy as jnp
from jax import lax
from jax.experimental import pallas as pl
from jax.experimental.pallas import tpu as pltpu
from jax.sharding import PartitionSpec as P


AXES = ("prompt", "feat")


def routes(move):
    pairs = []
    for x in range(4):
        for y in range(8):
            for z in range(8):
                for core in range(2):
                    pairs.append((flat(x, y, z, core), flat(*move(x, y, z, core))))
    return pairs


def flat(x, y, z, core):
    prompt = (x % 4) * 4 + y % 4
    feat = ((y // 4) % 2 * 8 + z % 8) * 2 + core
    return prompt * 32 + feat


UP_X = routes(lambda x, y, z, c: (x + 1, y, z, c))
DOWN_X = routes(lambda x, y, z, c: (x - 1, y, z, c))
RING_X = routes(lambda x, y, z, c: (x + (1 - 2 * c), y, z, c))
RING_Y = routes(lambda x, y, z, c: (x, y // 4 * 4 + (y + (1 - 2 * c)) % 4, z, c))
OTHER_Y = routes(lambda x, y, z, c: (x, (y + 4) % 8, z, c))
UP_Z = routes(lambda x, y, z, c: (x, y, z + 1, c))
DOWN_Z = routes(lambda x, y, z, c: (x, y, z - 1, c))
FAR_Z = routes(lambda x, y, z, c: (x, y, z + 4, c))
CORE = routes(lambda x, y, z, c: (x, y, z, 1 - c))


def send(value, pairs):
    return lax.ppermute(value, AXES, pairs)


def stack(*pieces):
    return jnp.concatenate(pieces, axis=0)


def turn(core, up, down):
    return jnp.where(core == 0, up, down)


def gather_rows(operands, into, sem, first):
    copies, at = [], 0
    for i, operand in enumerate(operands):
        size = operand.shape[0]
        copies.append(pltpu.make_async_copy(operand, into.at[pl.ds(at, size)], sem.at[first + i]))
        at += size
    for copy in copies:
        copy.start()
    return copies


def product_kernel(n_sources, n_targets, last, act_ref, order_ref, *refs):
    sources, targets = refs[:n_sources], refs[n_sources : n_sources + n_targets]
    refs = refs[n_sources + n_targets :]
    if last:
        row_at, before_ref = refs[:2]
        refs = refs[2:]
    out_ref, rows, cols, acc, sem = refs
    copies = gather_rows(sources, rows, sem, 0) + gather_rows(targets, cols, sem, n_sources)
    for copy in copies:
        copy.wait()
    depth = rows.shape[1]
    step = 768
    acc[...] = jnp.zeros_like(acc)

    @pl.loop(0, depth // step)
    def _(k):
        part = pl.ds(pl.multiple_of(k * step, step), step)
        acc[...] += lax.dot_general(
            rows[:, part], cols[:, part], (((1,), (1,)), ((), ())), preferred_element_type=jnp.float32
        )

    edges = (acc[...] * act_ref[...]).astype(jnp.bfloat16)
    placed = jnp.dot(edges, order_ref[...], preferred_element_type=jnp.float32)
    if not last:
        out_ref[...] = placed.astype(jnp.bfloat16)
        return
    placed = (placed + before_ref[...].astype(jnp.float32)).astype(jnp.bfloat16)
    for g in range(out_ref.shape[0] // 16):
        out_ref[pl.ds(pl.multiple_of(row_at[g], 16), 16), :] = placed[g * 16 : (g + 1) * 16]


def product(act, order, sources, targets, row_at=None, before=None):
    n_rows, (n_cols, n_out), depth = act.shape[0], order.shape, sources[0].shape[1]
    whole, smem, anywhere = (pl.BlockSpec(memory_space=m) for m in (pltpu.VMEM, pltpu.SMEM, pl.ANY))
    last = before is not None
    return pl.pallas_call(
        functools.partial(product_kernel, len(sources), len(targets), last),
        out_shape=jax.ShapeDtypeStruct((n_rows, n_out), jnp.bfloat16),
        in_specs=[whole, whole] + [anywhere] * (len(sources) + len(targets)) + ([smem, whole] if last else []),
        out_specs=whole,
        scratch_shapes=[
            pltpu.VMEM((n_rows, depth), jnp.bfloat16),
            pltpu.VMEM((n_cols, depth), jnp.bfloat16),
            pltpu.VMEM((n_rows, n_cols), jnp.float32),
            pltpu.SemaphoreType.DMA((len(sources) + len(targets),)),
        ],
        compiler_params=pltpu.CompilerParams(vmem_limit_bytes=32 << 20),
        name="last_product" if last else "first_product",
    )(act, order, *sources, *targets, *((row_at, before) if last else ()))


def edges_of(decoder, encoder, row_ids, counts, activity):
    slot_count = row_ids.shape[1]
    prompt, owner = lax.axis_index("prompt"), lax.axis_index("feat")
    core, chip = owner % 2, owner // 2
    half, z = chip // 8, chip % 8
    x, y = prompt // 4, prompt % 4
    sign = 1 - 2 * core

    picked_rows = jnp.take(decoder, row_ids[0], axis=0)
    live_count = lax.dynamic_index_in_dim(counts[0], owner, 0, keepdims=False)
    live_slots = jnp.arange(slot_count, dtype=jnp.int32) < live_count
    source_rows = jnp.where(live_slots[:, None], picked_rows, jnp.zeros((), picked_rows.dtype))

    y0 = encoder
    y1 = send(y0, RING_Y)
    y2 = send(y1, RING_Y)
    y3 = send(y2, RING_Y)
    a1, a2 = send(y0, UP_X), send(y0, DOWN_X)
    b1, b2 = send(y1, UP_X), send(y1, DOWN_X)
    c1, c2 = send(y2, UP_X), send(y2, DOWN_X)
    d1, d2 = send(y3, UP_X), send(y3, DOWN_X)
    a3 = send(turn(core, a1, a2), RING_X)
    f1 = send(a3, RING_Y)
    f2 = send(f1, RING_Y)
    d3 = send(turn(core, d1, d2), RING_X)

    own = lax.optimization_barrier(stack(source_rows, send(source_rows, OTHER_Y)))
    u1, w1 = send(own, UP_Z), send(own, DOWN_Z)
    u2, w2 = send(u1, UP_Z), send(w1, DOWN_Z)
    u3, w3 = send(u2, UP_Z), send(w2, DOWN_Z)
    zf = send(own, FAR_Z)
    near = stack(own, u1, w1, u2, w2)
    away = stack(u3, w3, zf)
    sources = [near, away, send(near, CORE), send(away, CORE)]

    hop = jnp.array([0, -1, 1, -2, 2, -3, 3, 4], jnp.int32)[None, :, None]
    side = jnp.arange(2, dtype=jnp.int32)[:, None, None]
    flip = jnp.arange(2, dtype=jnp.int32)[None, None, :]
    feat_from = ((half ^ flip) * 8 + (z + hop) % 8) * 2 + (core ^ side)
    group_from = feat_from.reshape(-1).astype(jnp.int32)
    x_from = (x + jnp.array([0, -1, 1, 2], jnp.int32)) % 4
    y_from = (y - sign * jnp.arange(4, dtype=jnp.int32)) % 4
    origin = x_from[None, :] * 4 + y_from[:, None]
    width = encoder.shape[0]
    first_of = origin.reshape(-1)[:12]
    last_of = origin.reshape(-1)[12:]
    act = activity[0].reshape(-1, slot_count)[group_from].reshape(-1, 1)

    def order(blocks):
        col_at = (blocks[:, None] * width + jnp.arange(width, dtype=jnp.int32)[None, :]).reshape(-1)
        place = jnp.arange(origin.size * width, dtype=jnp.int32)
        return (col_at[:, None] == place[None, :]).astype(jnp.bfloat16)

    part = product(act, order(first_of), sources, [y0, a1, a2, a3, y1, b1, b2, f1, y2, c1, c2, f2])
    edges = product(act, order(last_of), sources, [y3, d1, d2, d3], group_from * slot_count, part)
    return edges[None]


def solution(mesh):
    in_specs = (
        P("feat", None),
        P(("feat", "prompt"), None),
        P("prompt", "feat"),
        P("prompt", None),
        P("prompt", None),
    )
    out_specs = P("prompt", None, "feat")
    return jax.shard_map(edges_of, mesh=mesh, in_specs=in_specs, out_specs=out_specs, check_vma=False)
```

```python
import functools

import jax
import jax.numpy as jnp
from jax import lax
from jax.experimental import pallas as pl
from jax.experimental.pallas import tpu as pltpu
from jax.sharding import PartitionSpec as P


AXES = ("prompt", "feat")


def routes(move):
    pairs = []
    for x in range(4):
        for y in range(8):
            for z in range(8):
                for core in range(2):
                    pairs.append((flat(x, y, z, core), flat(*move(x, y, z, core))))
    return pairs


def flat(x, y, z, core):
    prompt = (x % 4) * 4 + y % 4
    feat = ((y // 4) % 2 * 8 + z % 8) * 2 + core
    return prompt * 32 + feat


UP_X = routes(lambda x, y, z, c: (x + 1, y, z, c))
DOWN_X = routes(lambda x, y, z, c: (x - 1, y, z, c))
RING_X = routes(lambda x, y, z, c: (x + (1 - 2 * c), y, z, c))
RING_Y = routes(lambda x, y, z, c: (x, y // 4 * 4 + (y + (1 - 2 * c)) % 4, z, c))
CORE = routes(lambda x, y, z, c: (x, y, z, 1 - c))
SAME_CORE = [list(range(core, 32, 2)) for core in range(2)]


def send(value, pairs):
    return lax.ppermute(value, AXES, pairs)


def turn(core, up, down):
    return jnp.where(core == 0, up, down)


def gather_rows(operands, into, sem, first):
    copies, at = [], 0
    for i, operand in enumerate(operands):
        size = operand.shape[0]
        copies.append(pltpu.make_async_copy(operand, into.at[pl.ds(at, size)], sem.at[first + i]))
        at += size
    for copy in copies:
        copy.start()
    return copies


def product_kernel(n_sources, n_targets, last, act_ref, order_ref, *refs):
    sources, targets = refs[:n_sources], refs[n_sources : n_sources + n_targets]
    refs = refs[n_sources + n_targets :]
    if last:
        row_at, *before_refs = refs[:3]
        refs = refs[3:]
    out_ref, rows, cols, acc, sem = refs
    copies = gather_rows(sources, rows, sem, 0) + gather_rows(targets, cols, sem, n_sources)
    for copy in copies:
        copy.wait()
    depth = rows.shape[1]
    step = 768
    acc[...] = jnp.zeros_like(acc)

    @pl.loop(0, depth // step)
    def _(k):
        part = pl.ds(pl.multiple_of(k * step, step), step)
        acc[...] += lax.dot_general(
            rows[:, part], cols[:, part], (((1,), (1,)), ((), ())), preferred_element_type=jnp.float32
        )

    edges = (acc[...] * act_ref[...]).astype(jnp.bfloat16)
    placed = jnp.dot(edges, order_ref[...], preferred_element_type=jnp.float32)
    if not last:
        out_ref[...] = placed.astype(jnp.bfloat16)
        return
    before = jnp.concatenate([before_ref[...] for before_ref in before_refs], axis=0)
    placed = (placed + before.astype(jnp.float32)).astype(jnp.bfloat16)
    for g in range(out_ref.shape[0] // 16):
        out_ref[pl.ds(pl.multiple_of(row_at[g], 16), 16), :] = placed[g * 16 : (g + 1) * 16]


def product(act, order, sources, targets, row_at=None, before=()):
    n_rows, (n_cols, n_out), depth = act.shape[0], order.shape, sources[0].shape[1]
    whole, smem, anywhere = (pl.BlockSpec(memory_space=m) for m in (pltpu.VMEM, pltpu.SMEM, pl.ANY))
    last = len(before) > 0
    return pl.pallas_call(
        functools.partial(product_kernel, len(sources), len(targets), last),
        out_shape=jax.ShapeDtypeStruct((n_rows, n_out), jnp.bfloat16),
        in_specs=[whole, whole] + [anywhere] * (len(sources) + len(targets)) + ([smem] + [whole] * len(before) if last else []),
        out_specs=whole,
        scratch_shapes=[
            pltpu.VMEM((n_rows, depth), jnp.bfloat16),
            pltpu.VMEM((n_cols, depth), jnp.bfloat16),
            pltpu.VMEM((n_rows, n_cols), jnp.float32),
            pltpu.SemaphoreType.DMA((len(sources) + len(targets),)),
        ],
        compiler_params=pltpu.CompilerParams(vmem_limit_bytes=32 << 20),
    )(act, order, *sources, *targets, *((row_at, *before) if last else ()))


def edges_of(decoder, encoder, row_ids, counts, activity):
    slot_count = row_ids.shape[1]
    prompt, owner = lax.axis_index("prompt"), lax.axis_index("feat")
    core = owner % 2
    x, y = prompt // 4, prompt % 4
    sign = 1 - 2 * core

    picked_rows = decoder.at[row_ids[0]].get(mode="promise_in_bounds")
    owners = jnp.arange(counts.shape[1], dtype=jnp.int32)
    live_count = jnp.sum(jnp.where(owners == owner, counts[0], 0))
    live_slots = jnp.arange(slot_count, dtype=jnp.int32) < live_count
    source_rows = jnp.where(live_slots[:, None], picked_rows, jnp.zeros((), picked_rows.dtype))
    mine = lax.all_gather(source_rows, "feat", axis=0, tiled=True, axis_index_groups=SAME_CORE)
    theirs = send(mine, CORE)

    y0 = encoder
    y1 = send(y0, RING_Y)
    y2 = send(y1, RING_Y)
    y3 = send(y2, RING_Y)
    a1, a2 = send(y0, UP_X), send(y0, DOWN_X)
    b1, b2 = send(y1, UP_X), send(y1, DOWN_X)
    c1, c2 = send(y2, UP_X), send(y2, DOWN_X)
    d1, d2 = send(y3, UP_X), send(y3, DOWN_X)
    a3 = send(turn(core, a1, a2), RING_X)
    f1 = send(a3, RING_Y)
    f2 = send(f1, RING_Y)
    d3 = send(turn(core, d1, d2), RING_X)

    side = jnp.arange(2, dtype=jnp.int32)[:, None]
    feat_from = jnp.arange(16, dtype=jnp.int32)[None, :] * 2 + (core ^ side)
    group_from = feat_from.reshape(-1).astype(jnp.int32)
    x_from = (x + jnp.array([0, -1, 1, 2], jnp.int32)) % 4
    y_from = (y - sign * jnp.arange(4, dtype=jnp.int32)) % 4
    origin = x_from[None, :] * 4 + y_from[:, None]
    width = encoder.shape[0]
    first_of = origin.reshape(-1)[:12]
    last_of = origin.reshape(-1)[12:]
    act = activity[0].reshape(-1, slot_count)[group_from].reshape(-1, 1)

    def order(blocks):
        col_at = (blocks[:, None] * width + jnp.arange(width, dtype=jnp.int32)[None, :]).reshape(-1)
        place = jnp.arange(origin.size * width, dtype=jnp.int32)
        return (col_at[:, None] == place[None, :]).astype(jnp.bfloat16)

    early = [y0, a1, a2, a3, y1, b1, b2, f1, y2, c1, c2, f2]
    half_rows = act.shape[0] // 2
    part_mine = product(act[:half_rows], order(first_of), [mine], early)
    part_theirs = product(act[half_rows:], order(first_of), [theirs], early)
    edges = product(
        act, order(last_of), [mine, theirs], [y3, d1, d2, d3],
        group_from * slot_count, (part_mine, part_theirs),
    )
    return edges[None]


def solution(mesh):
    in_specs = (
        P("feat", None),
        P(("feat", "prompt"), None),
        P("prompt", "feat"),
        P("prompt", None),
        P("prompt", None),
    )
    out_specs = P("prompt", None, "feat")
    return jax.shard_map(edges_of, mesh=mesh, in_specs=in_specs, out_specs=out_specs, check_vma=False)
```

```python
import functools

import jax
import jax.numpy as jnp
from jax import lax
from jax.experimental import pallas as pl
from jax.experimental.pallas import tpu as pltpu
from jax.sharding import PartitionSpec as P


AXES = ("prompt", "feat")


def routes(move):
    pairs = []
    for x in range(4):
        for y in range(8):
            for z in range(8):
                for core in range(2):
                    pairs.append((flat(x, y, z, core), flat(*move(x, y, z, core))))
    return pairs


def flat(x, y, z, core):
    prompt = (x % 4) * 4 + y % 4
    feat = ((y // 4) % 2 * 8 + z % 8) * 2 + core
    return prompt * 32 + feat


UP_X = routes(lambda x, y, z, c: (x + 1, y, z, c))
DOWN_X = routes(lambda x, y, z, c: (x - 1, y, z, c))
FAR_X = routes(lambda x, y, z, c: (x + 2, y, z, c))
RING_Y = routes(lambda x, y, z, c: (x, y // 4 * 4 + (y + (1 - 2 * c)) % 4, z, c))
OTHER_Y = routes(lambda x, y, z, c: (x, (y + 4) % 8, z, c))
UP_Z = routes(lambda x, y, z, c: (x, y, z + 1, c))
DOWN_Z = routes(lambda x, y, z, c: (x, y, z - 1, c))
CORE = routes(lambda x, y, z, c: (x, y, z, 1 - c))

HOPS_Z = (0, -1, 1, -2, 2, -3, 3, -4)
HOPS_X = (0, -1, 1, 2)
PARTS = 3


def send(value, pairs):
    return lax.ppermute(value, AXES, pairs)


def stack_kernel(*refs):
    operands, (out_ref, sem) = refs[:-2], refs[-2:]
    copies, at = [], 0
    for i, operand in enumerate(operands):
        size = operand.shape[0]
        copies.append(pltpu.make_async_copy(operand, out_ref.at[pl.ds(at, size)], sem.at[i]))
        at += size
    for copy in copies:
        copy.start()
    for copy in copies:
        copy.wait()


def stack(*pieces):
    n_rows = sum(piece.shape[0] for piece in pieces)
    anywhere = pl.BlockSpec(memory_space=pl.ANY)
    return pl.pallas_call(
        stack_kernel,
        out_shape=jax.ShapeDtypeStruct((n_rows, pieces[0].shape[1]), pieces[0].dtype),
        in_specs=[anywhere] * len(pieces),
        out_specs=anywhere,
        scratch_shapes=[pltpu.SemaphoreType.DMA((len(pieces),))],
    )(*pieces)


def place():
    prompt, owner = lax.axis_index("prompt"), lax.axis_index("feat")
    chip = owner // 2
    return prompt // 4, prompt % 4, chip // 8, chip % 8, owner % 2


def product_kernel(n_sources, n_targets, first_block, last, *refs):
    act_ref, refs = refs[0], refs[1:]
    if last:
        (rows, before_ref), refs = refs[:2], refs[2:]
        sources = ()
    else:
        sources, refs = refs[:n_sources], refs[n_sources:]
    targets, refs = refs[:n_targets], refs[n_targets:]
    if last:
        out_ref, cols, acc, order, act, sem = refs
    else:
        out_ref, rows, cols, acc, order, act, sem = refs
    depth = rows.shape[1]
    width = depth // PARTS

    def copies(part):
        at_depth = pl.ds(pl.multiple_of(part * width, 128), width)
        found, i = [], 0
        for into, operands in ((rows, sources), (cols, targets)):
            at = 0
            for operand in operands:
                size = operand.shape[0]
                found.append(
                    pltpu.make_async_copy(
                        operand.at[:, at_depth], into.at[pl.ds(at, size), at_depth], sem.at[part, i]
                    )
                )
                at += size
                i += 1
        return found

    for part in range(PARTS):
        for copy in copies(part):
            copy.start()

    x, y, half, z, core = place()
    slots = act_ref.shape[0] // 32
    row_at = []
    for side in range(2):
        for hop in HOPS_Z:
            for flip in range(2):
                feat = ((half ^ flip) * 8 + ((z + hop) & 7)) * 2 + (core ^ side)
                row_at.append(pl.multiple_of(feat * slots, slots))
    for g, at in enumerate(row_at):
        act[g * slots : (g + 1) * slots] = act_ref[pl.ds(at, slots)]
    block = out_ref.shape[1] // 16
    lane = lax.broadcasted_iota(jnp.int32, (block, out_ref.shape[1]), 1)
    line = lax.broadcasted_iota(jnp.int32, (block, out_ref.shape[1]), 0)
    for i in range(cols.shape[0] // block):
        step_y, hop = divmod(first_block + i, len(HOPS_X))
        origin = ((x + HOPS_X[hop]) & 3) * 4 + ((y - (1 - 2 * core) * step_y) & 3)
        order[i * block : (i + 1) * block] = jnp.where(lane == line + origin * block, 1.0, 0.0).astype(jnp.bfloat16)

    acc[...] = jnp.zeros_like(acc)

    @pl.loop(0, PARTS)
    def _(part):
        for copy in copies(part):
            copy.wait()
        at_depth = pl.ds(pl.multiple_of(part * width, 128), width)
        acc[...] += lax.dot_general(
            rows[:, at_depth], cols[:, at_depth], (((1,), (1,)), ((), ())), preferred_element_type=jnp.float32
        )

    edges = (acc[...] * act[...]).astype(jnp.bfloat16)
    placed = jnp.dot(edges, order[...], preferred_element_type=jnp.float32)
    if not last:
        out_ref[...] = placed.astype(jnp.bfloat16)
        return
    placed = (placed + before_ref[...].astype(jnp.float32)).astype(jnp.bfloat16)
    for g, at in enumerate(row_at):
        out_ref[pl.ds(at, slots), :] = placed[g * slots : (g + 1) * slots]


def product(act, first_block, sources, targets, rows=None, before=None):
    depth = targets[0].shape[1]
    n_rows = act.shape[0]
    n_cols, n_out = sum(t.shape[0] for t in targets), targets[0].shape[0] * 16
    whole, anywhere = pl.BlockSpec(memory_space=pltpu.VMEM), pl.BlockSpec(memory_space=pl.ANY)
    last = before is not None
    operands = (act, rows, before, *targets) if last else (act, *sources, *targets)
    edges_shape = jax.ShapeDtypeStruct((n_rows, n_out), jnp.bfloat16)
    rows_shape = jax.ShapeDtypeStruct((n_rows, depth), jnp.bfloat16)
    return pl.pallas_call(
        functools.partial(product_kernel, len(sources), len(targets), first_block, last),
        out_shape=edges_shape if last else (edges_shape, rows_shape),
        in_specs=[whole] * (3 if last else 1) + [anywhere] * (len(sources) + len(targets)),
        out_specs=whole if last else (whole, whole),
        scratch_shapes=[
            pltpu.VMEM((n_cols, depth), jnp.bfloat16),
            pltpu.VMEM((n_rows, n_cols), jnp.float32),
            pltpu.VMEM((n_cols, n_out), jnp.bfloat16),
            pltpu.VMEM((n_rows, 1), jnp.float32),
            pltpu.SemaphoreType.DMA((PARTS, len(sources) + len(targets))),
        ],
        compiler_params=pltpu.CompilerParams(vmem_limit_bytes=24 << 20),
    )(*operands)


def edges_of(decoder, encoder, row_ids, counts, activity):
    slot_count = row_ids.shape[1]
    owner = lax.axis_index("feat")

    picked_rows = decoder.at[row_ids[0]].get(mode="promise_in_bounds")
    owners = jnp.arange(counts.shape[1], dtype=jnp.int32)
    live_count = jnp.sum(jnp.where(owners == owner, counts[0], 0))
    live_slots = jnp.arange(slot_count, dtype=jnp.int32) < live_count
    source_rows = jnp.where(live_slots[:, None], picked_rows, jnp.zeros((), picked_rows.dtype))

    y0 = encoder
    y1 = send(y0, RING_Y)
    y2 = send(y1, RING_Y)
    y3 = send(y2, RING_Y)
    a1, a2, a3 = send(y0, UP_X), send(y0, DOWN_X), send(y0, FAR_X)
    b1, b2 = send(y1, UP_X), send(y1, DOWN_X)
    c1, c2 = send(y2, UP_X), send(y2, DOWN_X)
    d1, d2, d3 = send(y3, UP_X), send(y3, DOWN_X), send(y3, FAR_X)
    f1 = send(a3, RING_Y)
    f2 = send(f1, RING_Y)

    other = send(source_rows, OTHER_Y)
    own = jnp.concatenate([source_rows, other], axis=0)
    u1, w1 = send(own, UP_Z), send(own, DOWN_Z)
    u2, w2 = send(u1, UP_Z), send(w1, DOWN_Z)
    u3, w3 = send(u2, UP_Z), send(w2, DOWN_Z)
    u4 = send(u3, UP_Z)
    near = stack(own, u1, w1, u2, w2)
    away = stack(u3, w3, u4)
    sources = [near, away, send(near, CORE), send(away, CORE)]

    act = activity.reshape(-1, 1)
    part, rows = product(act, 0, sources, [y0, a1, a2, a3, y1, b1, b2, f1, y2, c1, c2, f2])
    edges = product(act, 12, [], [y3, d1, d2, d3], rows, part)
    return edges[None]


def solution(mesh):
    in_specs = (
        P("feat", None),
        P(("feat", "prompt"), None),
        P("prompt", "feat"),
        P("prompt", None),
        P("prompt", None),
    )
    out_specs = P("prompt", None, "feat")
    return jax.shard_map(edges_of, mesh=mesh, in_specs=in_specs, out_specs=out_specs, check_vma=False)
```

```python
import functools

import jax
import jax.numpy as jnp
from jax import lax
from jax.experimental import pallas as pl
from jax.experimental.pallas import tpu as pltpu
from jax.sharding import PartitionSpec as P


AXES = ("prompt", "feat")


def routes(move):
    pairs = []
    for x in range(4):
        for y in range(8):
            for z in range(8):
                for core in range(2):
                    pairs.append((flat(x, y, z, core), flat(*move(x, y, z, core))))
    return pairs


def flat(x, y, z, core):
    prompt = (x % 4) * 4 + y % 4
    feat = ((y // 4) % 2 * 8 + z % 8) * 2 + core
    return prompt * 32 + feat


UP_X = routes(lambda x, y, z, c: (x + 1, y, z, c))
DOWN_X = routes(lambda x, y, z, c: (x - 1, y, z, c))
FAR_X = routes(lambda x, y, z, c: (x + 2, y, z, c))
RING_Y = routes(lambda x, y, z, c: (x, y // 4 * 4 + (y + (1 - 2 * c)) % 4, z, c))
OTHER_Y = routes(lambda x, y, z, c: (x, (y + 4) % 8, z, c))
UP_Z = routes(lambda x, y, z, c: (x, y, z + 1, c))
DOWN_Z = routes(lambda x, y, z, c: (x, y, z - 1, c))
CORE = routes(lambda x, y, z, c: (x, y, z, 1 - c))

HOPS_Z = (0, -1, 1, -2, 2, -3, 3, -4)
HOPS_X = (0, -1, 1, 2)
PARTS = 3


def send(value, pairs):
    return lax.ppermute(value, AXES, pairs)


def stack_kernel(*refs):
    operands, (out_ref, sem) = refs[:-2], refs[-2:]
    copies, at = [], 0
    for i, operand in enumerate(operands):
        size = operand.shape[0]
        copies.append(pltpu.make_async_copy(operand, out_ref.at[pl.ds(at, size)], sem.at[i]))
        at += size
    for copy in copies:
        copy.start()
    for copy in copies:
        copy.wait()


def stack(*pieces):
    n_rows = sum(piece.shape[0] for piece in pieces)
    return pl.pallas_call(
        stack_kernel,
        out_shape=jax.ShapeDtypeStruct((n_rows, pieces[0].shape[1]), pieces[0].dtype),
        in_specs=[pl.BlockSpec(memory_space=pl.ANY)] * len(pieces),
        out_specs=pl.BlockSpec(memory_space=pltpu.VMEM),
        scratch_shapes=[pltpu.SemaphoreType.DMA((len(pieces),))],
    )(*pieces)


def place():
    prompt, owner = lax.axis_index("prompt"), lax.axis_index("feat")
    chip = owner // 2
    return prompt // 4, prompt % 4, chip // 8, chip % 8, owner % 2


def product_kernel(n_sources, n_targets, first_block, last, *refs):
    act_ref, refs = refs[0], refs[1:]
    if last:
        (rows, before_ref), refs = refs[:2], refs[2:]
        sources = ()
    else:
        sources, refs = refs[:n_sources], refs[n_sources:]
    targets, refs = refs[:n_targets], refs[n_targets:]
    if last:
        out_ref, cols, acc, order, act, sem = refs
    else:
        out_ref, rows, cols, acc, order, act, sem = refs
    depth = rows.shape[1]
    width = depth // PARTS

    def copies(part):
        at_depth = pl.ds(pl.multiple_of(part * width, 128), width)
        found, i = [], 0
        for into, operands in ((rows, sources), (cols, targets)):
            at = 0
            for operand in operands:
                size = operand.shape[0]
                found.append(
                    pltpu.make_async_copy(
                        operand.at[:, at_depth], into.at[pl.ds(at, size), at_depth], sem.at[part, i]
                    )
                )
                at += size
                i += 1
        return found

    for part in range(PARTS):
        for copy in copies(part):
            copy.start()

    x, y, half, z, core = place()
    slots = act_ref.shape[0] // 32
    row_at = []
    for side in range(2):
        for hop in HOPS_Z:
            for flip in range(2):
                feat = ((half ^ flip) * 8 + ((z + hop) & 7)) * 2 + (core ^ side)
                row_at.append(pl.multiple_of(feat * slots, slots))
    for g, at in enumerate(row_at):
        act[g * slots : (g + 1) * slots] = act_ref[pl.ds(at, slots)]
    block = out_ref.shape[1] // 16
    lane = lax.broadcasted_iota(jnp.int32, (block, out_ref.shape[1]), 1)
    line = lax.broadcasted_iota(jnp.int32, (block, out_ref.shape[1]), 0)
    for i in range(cols.shape[0] // block):
        step_y, hop = divmod(first_block + i, len(HOPS_X))
        origin = ((x + HOPS_X[hop]) & 3) * 4 + ((y - (1 - 2 * core) * step_y) & 3)
        order[i * block : (i + 1) * block] = jnp.where(lane == line + origin * block, 1.0, 0.0).astype(jnp.bfloat16)

    acc[...] = jnp.zeros_like(acc)

    @pl.loop(0, PARTS)
    def _(part):
        for copy in copies(part):
            copy.wait()
        at_depth = pl.ds(pl.multiple_of(part * width, 128), width)
        acc[...] += lax.dot_general(
            rows[:, at_depth], cols[:, at_depth], (((1,), (1,)), ((), ())), preferred_element_type=jnp.float32
        )

    edges = (acc[...] * act[...]).astype(jnp.bfloat16)
    placed = jnp.dot(edges, order[...], preferred_element_type=jnp.float32)
    if not last:
        out_ref[...] = placed.astype(jnp.bfloat16)
        return
    placed = (placed + before_ref[...].astype(jnp.float32)).astype(jnp.bfloat16)
    for g, at in enumerate(row_at):
        out_ref[pl.ds(at, slots), :] = placed[g * slots : (g + 1) * slots]


def product(act, first_block, sources, targets, rows=None, before=None):
    depth = targets[0].shape[1]
    n_rows = act.shape[0]
    n_cols, n_out = sum(t.shape[0] for t in targets), targets[0].shape[0] * 16
    whole, anywhere = pl.BlockSpec(memory_space=pltpu.VMEM), pl.BlockSpec(memory_space=pl.ANY)
    last = before is not None
    operands = (act, rows, before, *targets) if last else (act, *sources, *targets)
    edges_shape = jax.ShapeDtypeStruct((n_rows, n_out), jnp.bfloat16)
    rows_shape = jax.ShapeDtypeStruct((n_rows, depth), jnp.bfloat16)
    return pl.pallas_call(
        functools.partial(product_kernel, len(sources), len(targets), first_block, last),
        out_shape=edges_shape if last else (edges_shape, rows_shape),
        in_specs=[whole] * (3 if last else 1) + [anywhere] * (len(sources) + len(targets)),
        out_specs=whole if last else (whole, whole),
        scratch_shapes=[
            pltpu.VMEM((n_cols, depth), jnp.bfloat16),
            pltpu.VMEM((n_rows, n_cols), jnp.float32),
            pltpu.VMEM((n_cols, n_out), jnp.bfloat16),
            pltpu.VMEM((n_rows, 1), jnp.float32),
            pltpu.SemaphoreType.DMA((PARTS, len(sources) + len(targets))),
        ],
        compiler_params=pltpu.CompilerParams(vmem_limit_bytes=24 << 20),
    )(*operands)


def edges_of(decoder, encoder, row_ids, counts, activity):
    slot_count = row_ids.shape[1]
    owner = lax.axis_index("feat")

    picked_rows = decoder.at[row_ids[0]].get(mode="promise_in_bounds")
    owners = jnp.arange(counts.shape[1], dtype=jnp.int32)
    live_count = jnp.sum(jnp.where(owners == owner, counts[0], 0))
    live_slots = jnp.arange(slot_count, dtype=jnp.int32) < live_count
    source_rows = jnp.where(live_slots[:, None], picked_rows, jnp.zeros((), picked_rows.dtype))

    y0 = encoder
    y1 = send(y0, RING_Y)
    y2 = send(y1, RING_Y)
    y3 = send(y2, RING_Y)
    a1, a2, a3 = send(y0, UP_X), send(y0, DOWN_X), send(y0, FAR_X)
    b1, b2 = send(y1, UP_X), send(y1, DOWN_X)
    c1, c2 = send(y2, UP_X), send(y2, DOWN_X)
    d1, d2, d3 = send(y3, UP_X), send(y3, DOWN_X), send(y3, FAR_X)
    f1 = send(a3, RING_Y)
    f2 = send(f1, RING_Y)

    other = send(source_rows, OTHER_Y)
    own = jnp.concatenate([source_rows, other], axis=0)
    u1, w1 = send(own, UP_Z), send(own, DOWN_Z)
    u2, w2 = send(u1, UP_Z), send(w1, DOWN_Z)
    u3, w3 = send(u2, UP_Z), send(w2, DOWN_Z)
    u4 = send(u3, UP_Z)
    near = stack(own, u1, w1, u2, w2)
    away = stack(u3, w3, u4)
    sources = [near, away, send(near, CORE), send(away, CORE)]

    act = activity.reshape(-1, 1)
    part, rows = product(act, 0, sources, [y0, a1, a2, a3, y1, b1, b2, f1, y2, c1, c2, f2])
    edges = product(act, 12, [], [y3, d1, d2, d3], rows, part)
    return edges[None]


def solution(mesh):
    in_specs = (
        P("feat", None),
        P(("feat", "prompt"), None),
        P("prompt", "feat"),
        P("prompt", None),
        P("prompt", None),
    )
    out_specs = P("prompt", None, "feat")
    return jax.shard_map(edges_of, mesh=mesh, in_specs=in_specs, out_specs=out_specs, check_vma=False)
```

```python
import functools

import jax
import jax.numpy as jnp
from jax import lax
from jax.experimental import pallas as pl
from jax.experimental.pallas import tpu as pltpu
from jax.sharding import PartitionSpec as P


AXES = ("prompt", "feat")


def routes(move):
    pairs = []
    for x in range(4):
        for y in range(8):
            for z in range(8):
                for core in range(2):
                    pairs.append((flat(x, y, z, core), flat(*move(x, y, z, core))))
    return pairs


def flat(x, y, z, core):
    prompt = (x % 4) * 4 + y % 4
    feat = ((y // 4) % 2 * 8 + z % 8) * 2 + core
    return prompt * 32 + feat


UP_X = routes(lambda x, y, z, c: (x + 1, y, z, c))
DOWN_X = routes(lambda x, y, z, c: (x - 1, y, z, c))
RING_Y = routes(lambda x, y, z, c: (x, y // 4 * 4 + (y + (1 - 2 * c)) % 4, z, c))
OTHER_Y = routes(lambda x, y, z, c: (x, (y + 4) % 8, z, c))
UP_Z = routes(lambda x, y, z, c: (x, y, z + 1, c))
DOWN_Z = routes(lambda x, y, z, c: (x, y, z - 1, c))
CORE = routes(lambda x, y, z, c: (x, y, z, 1 - c))
ROWS_X = [[x * 4 + y for x in range(4)] for y in range(4)]

HOPS_Z = (0, -1, 1, -2, 2, -3, 3, -4)
HOPS_X = (0, -1, 1, 2)
PARTS = 3


def send(value, pairs):
    return lax.ppermute(value, AXES, pairs)


def share(value):
    copies = jnp.broadcast_to(value[None], (4,) + value.shape)
    return lax.all_to_all(copies, "prompt", 0, 0, axis_index_groups=ROWS_X, tiled=True)


def stack_kernel(*refs):
    operands, (out_ref, sem) = refs[:-2], refs[-2:]
    copies, at = [], 0
    for i, operand in enumerate(operands):
        size = operand.shape[0]
        copies.append(pltpu.make_async_copy(operand, out_ref.at[pl.ds(at, size)], sem.at[i]))
        at += size
    for copy in copies:
        copy.start()
    for copy in copies:
        copy.wait()


def stack(*pieces):
    n_rows = sum(piece.shape[0] for piece in pieces)
    return pl.pallas_call(
        stack_kernel,
        out_shape=jax.ShapeDtypeStruct((n_rows, pieces[0].shape[1]), pieces[0].dtype),
        in_specs=[pl.BlockSpec(memory_space=pl.ANY)] * len(pieces),
        out_specs=pl.BlockSpec(memory_space=pltpu.VMEM),
        scratch_shapes=[pltpu.SemaphoreType.DMA((len(pieces),))],
    )(*pieces)


def place():
    prompt, owner = lax.axis_index("prompt"), lax.axis_index("feat")
    chip = owner // 2
    return prompt // 4, prompt % 4, chip // 8, chip % 8, owner % 2


def product_kernel(n_sources, act_ref, *refs):
    operands, (out_ref, rows, cols, acc, order, act, sem) = refs[:-7], refs[-7:]
    sources, targets = operands[:n_sources], operands[n_sources:]
    width = rows.shape[1] // PARTS

    def copies(part):
        at_depth = pl.ds(pl.multiple_of(part * width, 128), width)
        found, i = [], 0
        for into, pieces in ((rows, sources), (cols, targets)):
            at = 0
            for piece in pieces:
                size = piece.shape[0]
                found.append(
                    pltpu.make_async_copy(
                        piece.at[:, at_depth], into.at[pl.ds(at, size), at_depth], sem.at[part, i]
                    )
                )
                at += size
                i += 1
        return found

    for part in range(PARTS):
        for copy in copies(part):
            copy.start()

    x, y, half, z, core = place()
    slots = act_ref.shape[0] // 32
    row_at = []
    for side in range(2):
        for hop in HOPS_Z:
            for flip in range(2):
                feat = ((half ^ flip) * 8 + ((z + hop) & 7)) * 2 + (core ^ side)
                row_at.append(pl.multiple_of(feat * slots, slots))
    for g, at in enumerate(row_at):
        act[g * slots : (g + 1) * slots] = act_ref[pl.ds(at, slots)]
    block = out_ref.shape[1] // 16
    lane = lax.broadcasted_iota(jnp.int32, (block, out_ref.shape[1]), 1)
    line = lax.broadcasted_iota(jnp.int32, (block, out_ref.shape[1]), 0)
    for i in range(16):
        step_y, step_x = divmod(i, 4)
        x_from = step_x if step_y in (0, 3) else (x + HOPS_X[step_x]) & 3
        origin = x_from * 4 + ((y - (1 - 2 * core) * step_y) & 3)
        order[i * block : (i + 1) * block] = jnp.where(lane == line + origin * block, 1.0, 0.0).astype(jnp.bfloat16)

    acc[...] = jnp.zeros_like(acc)

    @pl.loop(0, PARTS)
    def _(part):
        for copy in copies(part):
            copy.wait()
        at_depth = pl.ds(pl.multiple_of(part * width, 128), width)
        acc[...] += lax.dot_general(
            rows[:, at_depth], cols[:, at_depth], (((1,), (1,)), ((), ())), preferred_element_type=jnp.float32
        )

    edges = (acc[...] * act[...]).astype(jnp.bfloat16)
    placed = jnp.dot(edges, order[...], preferred_element_type=jnp.float32).astype(jnp.bfloat16)
    for g, at in enumerate(row_at):
        out_ref[pl.ds(at, slots), :] = placed[g * slots : (g + 1) * slots]


def product(act, sources, targets):
    depth = targets[0].shape[1]
    n_rows, n_cols = act.shape[0], sum(t.shape[0] for t in targets)
    whole, anywhere = pl.BlockSpec(memory_space=pltpu.VMEM), pl.BlockSpec(memory_space=pltpu.HBM)
    return pl.pallas_call(
        functools.partial(product_kernel, len(sources)),
        out_shape=jax.ShapeDtypeStruct((n_rows, n_cols), jnp.bfloat16),
        in_specs=[whole] + [anywhere] * (len(sources) + len(targets)),
        out_specs=whole,
        scratch_shapes=[
            pltpu.VMEM((n_rows, depth), jnp.bfloat16),
            pltpu.VMEM((n_cols, depth), jnp.bfloat16),
            pltpu.VMEM((n_rows, n_cols), jnp.float32),
            pltpu.VMEM((n_cols, n_cols), jnp.bfloat16),
            pltpu.VMEM((n_rows, 1), jnp.float32),
            pltpu.SemaphoreType.DMA((PARTS, len(sources) + len(targets))),
        ],
        compiler_params=pltpu.CompilerParams(vmem_limit_bytes=28 << 20),
        name="product",
    )(act, *sources, *targets)


def edges_of(decoder, encoder, row_ids, counts, activity):
    slot_count = row_ids.shape[1]
    owner = lax.axis_index("feat")

    picked_rows = decoder.at[row_ids[0]].get(mode="promise_in_bounds")
    owners = jnp.arange(counts.shape[1], dtype=jnp.int32)
    live_count = jnp.sum(jnp.where(owners == owner, counts[0], 0))
    live_slots = jnp.arange(slot_count, dtype=jnp.int32) < live_count
    source_rows = jnp.where(live_slots[:, None], picked_rows, jnp.zeros((), picked_rows.dtype))

    y0 = encoder
    y1 = send(y0, RING_Y)
    y2 = send(y1, RING_Y)
    y3 = send(y2, RING_Y)
    width = y0.shape[0]
    aa, dd = share(y0), share(y3)
    b1, b2 = send(y1, UP_X), send(y1, DOWN_X)
    c1, c2 = send(y2, UP_X), send(y2, DOWN_X)
    far = lax.dynamic_index_in_dim(aa, (lax.axis_index("prompt") // 4 + 2) % 4, 0, keepdims=False)
    f1 = send(far, RING_Y)
    f2 = send(f1, RING_Y)

    other = send(source_rows, OTHER_Y)
    own = jnp.concatenate([source_rows, other], axis=0)
    u1, w1 = send(own, UP_Z), send(own, DOWN_Z)
    u2, w2 = send(u1, UP_Z), send(w1, DOWN_Z)
    u3, w3 = send(u2, UP_Z), send(w2, DOWN_Z)
    u4 = send(u3, UP_Z)
    near = stack(own, u1, w1, u2, w2)
    away = stack(u3, w3, u4)
    sources = [near, away, send(near, CORE), send(away, CORE)]

    targets = [aa.reshape(4 * width, -1), y1, b1, b2, f1, y2, c1, c2, f2, dd.reshape(4 * width, -1)]
    return product(activity.reshape(-1, 1), sources, targets)[None]


def solution(mesh):
    in_specs = (
        P("feat", None),
        P(("feat", "prompt"), None),
        P("prompt", "feat"),
        P("prompt", None),
        P("prompt", None),
    )
    out_specs = P("prompt", None, "feat")
    return jax.shard_map(edges_of, mesh=mesh, in_specs=in_specs, out_specs=out_specs, check_vma=False)
```

```python
import functools

import jax
import jax.numpy as jnp
from jax import lax
from jax.experimental import pallas as pl
from jax.experimental.pallas import tpu as pltpu
from jax.sharding import PartitionSpec as P


AXES = ("prompt", "feat")


def routes(move):
    pairs = []
    for x in range(4):
        for y in range(8):
            for z in range(8):
                for core in range(2):
                    pairs.append((flat(x, y, z, core), flat(*move(x, y, z, core))))
    return pairs


def flat(x, y, z, core):
    prompt = (x % 4) * 4 + y % 4
    feat = ((y // 4) % 2 * 8 + z % 8) * 2 + core
    return prompt * 32 + feat


UP_X = routes(lambda x, y, z, c: (x + 1, y, z, c))
DOWN_X = routes(lambda x, y, z, c: (x - 1, y, z, c))
RING_Y = routes(lambda x, y, z, c: (x, y // 4 * 4 + (y + (1 - 2 * c)) % 4, z, c))
OTHER_Y = routes(lambda x, y, z, c: (x, (y + 4) % 8, z, c))
UP_Z = routes(lambda x, y, z, c: (x, y, z + 1, c))
DOWN_Z = routes(lambda x, y, z, c: (x, y, z - 1, c))
CORE = routes(lambda x, y, z, c: (x, y, z, 1 - c))
ROWS_X = [[x * 4 + y for x in range(4)] for y in range(4)]

HOPS_Z = (0, -1, 1, -2, 2, -3, 3, -4)
ALL_X = tuple((None, x) for x in range(4))
BLOCKS = (
    *((0, *at) for at in ALL_X),
    *((step, hop, None) for hop in (0, -1, 1, 2) for step in (1, 2)),
    *((3, *at) for at in ALL_X),
)
PARTS = 7


def send(value, pairs):
    return lax.ppermute(value, AXES, pairs)


def spread_kernel(value_ref, out_ref, held, sem):
    copy = pltpu.make_async_copy(value_ref, held, sem.at[4])
    copy.start()
    copy.wait()
    copies = [pltpu.make_async_copy(held, out_ref.at[i], sem.at[i]) for i in range(4)]
    for copy in copies:
        copy.start()
    for copy in copies:
        copy.wait()


def share(value):
    copies = pl.pallas_call(
        spread_kernel,
        out_shape=jax.ShapeDtypeStruct((4,) + value.shape, value.dtype),
        in_specs=[pl.BlockSpec(memory_space=pl.ANY)],
        out_specs=pl.BlockSpec(memory_space=pl.ANY),
        scratch_shapes=[pltpu.VMEM(value.shape, value.dtype), pltpu.SemaphoreType.DMA((5,))],
        name="spread",
    )(value)
    return lax.all_to_all(copies, "prompt", 0, 0, axis_index_groups=ROWS_X, tiled=True)


def stack_kernel(*refs):
    operands, (out_ref, held, sem) = refs[:-3], refs[-3:]
    inward, outward, at = [], [], 0
    for i, operand in enumerate(operands):
        lines = pl.ds(at, operand.shape[0])
        inward.append(pltpu.make_async_copy(operand, held.at[lines], sem.at[0, i]))
        outward.append(pltpu.make_async_copy(held.at[lines], out_ref.at[lines], sem.at[1, i]))
        at += operand.shape[0]
    for copy in inward:
        copy.start()
    for copy, onward in zip(inward, outward):
        copy.wait()
        onward.start()
    for copy in outward:
        copy.wait()


def stack(*pieces):
    shape = (sum(piece.shape[0] for piece in pieces), pieces[0].shape[1])
    return pl.pallas_call(
        stack_kernel,
        out_shape=jax.ShapeDtypeStruct(shape, pieces[0].dtype),
        in_specs=[pl.BlockSpec(memory_space=pl.ANY)] * len(pieces),
        out_specs=pl.BlockSpec(memory_space=pl.ANY),
        scratch_shapes=[pltpu.VMEM(shape, pieces[0].dtype), pltpu.SemaphoreType.DMA((2, len(pieces)))],
    )(*pieces)


def place():
    prompt, owner = lax.axis_index("prompt"), lax.axis_index("feat")
    chip = owner // 2
    return prompt // 4, prompt % 4, chip // 8, chip % 8, owner % 2


def product_kernel(n_sources, act_ref, *refs):
    operands, (out_ref, rows, cols, acc, order, act, sem) = refs[:-7], refs[-7:]
    sources, targets = operands[:n_sources], operands[n_sources:]
    width = rows.shape[1] // PARTS

    def copies(part):
        at_depth = pl.ds(pl.multiple_of(part * width, 128), width)
        found, i = [], 0
        for into, pieces in ((rows, sources), (cols, targets)):
            at = 0
            for piece in pieces:
                size = piece.shape[0]
                found.append(
                    pltpu.make_async_copy(
                        piece.at[:, at_depth], into.at[pl.ds(at, size), at_depth], sem.at[part, i]
                    )
                )
                at += size
                i += 1
        return found

    for part in range(PARTS):
        for copy in copies(part):
            copy.start()

    x, y, half, z, core = place()
    slots = act_ref.shape[0] // 32
    row_at = []
    for side in range(2):
        for hop in HOPS_Z:
            for flip in range(2):
                feat = ((half ^ flip) * 8 + ((z + hop) & 7)) * 2 + (core ^ side)
                row_at.append(pl.multiple_of(feat * slots, slots))
    for g, at in enumerate(row_at):
        act[g * slots : (g + 1) * slots] = act_ref[pl.ds(at, slots)]
    block = out_ref.shape[1] // 16
    lane = lax.broadcasted_iota(jnp.int32, (block, out_ref.shape[1]), 1)
    line = lax.broadcasted_iota(jnp.int32, (block, out_ref.shape[1]), 0)
    for i, (step_y, hop, x_there) in enumerate(BLOCKS):
        x_from = x_there if hop is None else (x + hop) & 3
        origin = x_from * 4 + ((y - (1 - 2 * core) * step_y) & 3)
        order[i * block : (i + 1) * block] = jnp.where(lane == line + origin * block, 1.0, 0.0).astype(jnp.bfloat16)

    acc[...] = jnp.zeros_like(acc)

    @pl.loop(0, PARTS)
    def _(part):
        for copy in copies(part):
            copy.wait()
        at_depth = pl.ds(pl.multiple_of(part * width, 128), width)
        acc[...] += lax.dot_general(
            rows[:, at_depth], cols[:, at_depth], (((1,), (1,)), ((), ())), preferred_element_type=jnp.float32
        )

    edges = (acc[...] * act[...]).astype(jnp.bfloat16)
    placed = jnp.dot(edges, order[...], preferred_element_type=jnp.float32).astype(jnp.bfloat16)
    for g, at in enumerate(row_at):
        out_ref[pl.ds(at, slots), :] = placed[g * slots : (g + 1) * slots]


def product(act, sources, targets):
    depth = targets[0].shape[1]
    n_rows, n_cols = act.shape[0], sum(t.shape[0] for t in targets)
    whole, anywhere = pl.BlockSpec(memory_space=pltpu.VMEM), pl.BlockSpec(memory_space=pltpu.HBM)
    return pl.pallas_call(
        functools.partial(product_kernel, len(sources)),
        out_shape=jax.ShapeDtypeStruct((n_rows, n_cols), jnp.bfloat16),
        in_specs=[whole] + [anywhere] * (len(sources) + len(targets)),
        out_specs=whole,
        scratch_shapes=[
            pltpu.VMEM((n_rows, depth), jnp.bfloat16),
            pltpu.VMEM((n_cols, depth), jnp.bfloat16),
            pltpu.VMEM((n_rows, n_cols), jnp.float32),
            pltpu.VMEM((n_cols, n_cols), jnp.bfloat16),
            pltpu.VMEM((n_rows, 1), jnp.float32),
            pltpu.SemaphoreType.DMA((PARTS, len(sources) + len(targets))),
        ],
        compiler_params=pltpu.CompilerParams(vmem_limit_bytes=28 << 20),
        name="product",
    )(act, *sources, *targets)


def edges_of(decoder, encoder, row_ids, counts, activity):
    slot_count = row_ids.shape[1]
    owner = lax.axis_index("feat")

    picked_rows = decoder.at[row_ids[0]].get(mode="promise_in_bounds")
    owners = jnp.arange(counts.shape[1], dtype=jnp.int32)
    live_count = jnp.sum(jnp.where(owners == owner, counts[0], 0))
    live_slots = jnp.arange(slot_count, dtype=jnp.int32) < live_count
    source_rows = jnp.where(live_slots[:, None], picked_rows, jnp.zeros((), picked_rows.dtype))

    y0 = encoder
    y1 = send(y0, RING_Y)
    y2 = send(y1, RING_Y)
    y3 = send(y2, RING_Y)
    width = y0.shape[0]
    aa, dd = share(y0), share(y3)
    both = jnp.concatenate([y1, y2], axis=0)
    m1, m2 = send(both, UP_X), send(both, DOWN_X)
    far = lax.dynamic_index_in_dim(aa, (lax.axis_index("prompt") // 4 + 2) % 4, 0, keepdims=False)
    f1 = send(far, RING_Y)
    f2 = send(f1, RING_Y)

    other = send(source_rows, OTHER_Y)
    own = jnp.concatenate([source_rows, other], axis=0)
    u1, w1 = send(own, UP_Z), send(own, DOWN_Z)
    u2, w2 = send(u1, UP_Z), send(w1, DOWN_Z)
    u3, w3 = send(u2, UP_Z), send(w2, DOWN_Z)
    u4 = send(u3, UP_Z)
    near = stack(own, u1, w1, u2, w2)
    away = stack(u3, w3, u4)
    sources = [own, u1, w1, u2, w2, u3, w3, u4, send(near, CORE), send(away, CORE)]

    targets = [aa.reshape(4 * width, -1), y1, y2, m1, m2, f1, f2, dd.reshape(4 * width, -1)]
    return product(activity.reshape(-1, 1), sources, targets)[None]


def solution(mesh):
    in_specs = (
        P("feat", None),
        P(("feat", "prompt"), None),
        P("prompt", "feat"),
        P("prompt", None),
        P("prompt", None),
    )
    out_specs = P("prompt", None, "feat")
    return jax.shard_map(edges_of, mesh=mesh, in_specs=in_specs, out_specs=out_specs, check_vma=False)
```

```python
import functools

import jax
import jax.numpy as jnp
from jax import lax
from jax.experimental import pallas as pl
from jax.experimental.pallas import tpu as pltpu
from jax.sharding import PartitionSpec as P


AXES = ("prompt", "feat")


def routes(move):
    pairs = []
    for x in range(4):
        for y in range(8):
            for z in range(8):
                for core in range(2):
                    pairs.append((flat(x, y, z, core), flat(*move(x, y, z, core))))
    return pairs


def flat(x, y, z, core):
    prompt = (x % 4) * 4 + y % 4
    feat = ((y // 4) % 2 * 8 + z % 8) * 2 + core
    return prompt * 32 + feat


UP_X = routes(lambda x, y, z, c: (x + 1, y, z, c))
DOWN_X = routes(lambda x, y, z, c: (x - 1, y, z, c))
RING_Y = routes(lambda x, y, z, c: (x, y // 4 * 4 + (y + (1 - 2 * c)) % 4, z, c))
OTHER_Y = routes(lambda x, y, z, c: (x, (y + 4) % 8, z, c))
CORE = routes(lambda x, y, z, c: (x, y, z, 1 - c))
ROWS_X = [[x * 4 + y for x in range(4)] for y in range(4)]
ROWS_Z = [[(half * 8 + z) * 2 + core for z in range(8)] for half in range(2) for core in range(2)]

HOPS_X = (0, -1, 1, 2)
PARTS = 3


def send(value, pairs):
    return lax.ppermute(value, AXES, pairs)


def share(value):
    copies = jnp.broadcast_to(value[None], (4,) + value.shape)
    return lax.all_to_all(copies, "prompt", 0, 0, axis_index_groups=ROWS_X, tiled=True)


def place():
    prompt, owner = lax.axis_index("prompt"), lax.axis_index("feat")
    chip = owner // 2
    return prompt // 4, prompt % 4, chip // 8, chip % 8, owner % 2


def rows_of(side, place_of, slots):
    _, _, half, _, core = place_of
    feats = [((half ^ flip) * 8 + z) * 2 + (core ^ side) for z in range(8) for flip in range(2)]
    return [pl.multiple_of(feat * slots, slots) for feat in feats]


def product_kernel(side, act_ref, *refs):
    operands, (out_ref, rows, cols, acc, order, act, sem) = refs[:-7], refs[-7:]
    if side:
        before_ref, operands = operands[0], operands[1:]
    sources, targets = operands[:1], operands[1:]
    width = rows.shape[1] // PARTS

    def copies(part):
        at_depth = pl.ds(pl.multiple_of(part * width, 128), width)
        found, i = [], 0
        for into, pieces in ((rows, sources), (cols, targets)):
            at = 0
            for piece in pieces:
                size = piece.shape[0]
                found.append(
                    pltpu.make_async_copy(
                        piece.at[:, at_depth], into.at[pl.ds(at, size), at_depth], sem.at[part, i]
                    )
                )
                at += size
                i += 1
        return found

    for part in range(PARTS):
        for copy in copies(part):
            copy.start()

    here = place()
    x, y, _, _, core = here
    slots = act_ref.shape[0] // 32
    row_at = rows_of(side, here, slots)
    for g, at in enumerate(row_at):
        act[g * slots : (g + 1) * slots] = act_ref[pl.ds(at, slots)]
    block = out_ref.shape[1] // 16
    lane = lax.broadcasted_iota(jnp.int32, (block, out_ref.shape[1]), 1)
    line = lax.broadcasted_iota(jnp.int32, (block, out_ref.shape[1]), 0)
    for i in range(16):
        step_y, step_x = divmod(i, 4)
        x_from = step_x if step_y in (0, 3) else (x + HOPS_X[step_x]) & 3
        origin = x_from * 4 + ((y - (1 - 2 * core) * step_y) & 3)
        order[i * block : (i + 1) * block] = jnp.where(lane == line + origin * block, 1.0, 0.0).astype(jnp.bfloat16)

    acc[...] = jnp.zeros_like(acc)

    @pl.loop(0, PARTS)
    def _(part):
        for copy in copies(part):
            copy.wait()
        at_depth = pl.ds(pl.multiple_of(part * width, 128), width)
        acc[...] += lax.dot_general(
            rows[:, at_depth], cols[:, at_depth], (((1,), (1,)), ((), ())), preferred_element_type=jnp.float32
        )

    edges = (acc[...] * act[...]).astype(jnp.bfloat16)
    placed = jnp.dot(edges, order[...], preferred_element_type=jnp.float32).astype(jnp.bfloat16)
    if not side:
        out_ref[...] = placed
        return
    for g, (at, before_at) in enumerate(zip(row_at, rows_of(0, here, slots))):
        out_ref[pl.ds(at, slots), :] = placed[g * slots : (g + 1) * slots]
        out_ref[pl.ds(before_at, slots), :] = before_ref[g * slots : (g + 1) * slots, :]


def product(act, rows, targets, before=None):
    (n_rows, depth), n_cols = rows.shape, sum(t.shape[0] for t in targets)
    whole, anywhere = pl.BlockSpec(memory_space=pltpu.VMEM), pl.BlockSpec(memory_space=pl.ANY)
    side = 0 if before is None else 1
    return pl.pallas_call(
        functools.partial(product_kernel, side),
        out_shape=jax.ShapeDtypeStruct((n_rows * (1 + side), n_cols), jnp.bfloat16),
        in_specs=[whole] * (1 + side) + [anywhere] * (1 + len(targets)),
        out_specs=whole,
        scratch_shapes=[
            pltpu.VMEM((n_rows, depth), jnp.bfloat16),
            pltpu.VMEM((n_cols, depth), jnp.bfloat16),
            pltpu.VMEM((n_rows, n_cols), jnp.float32),
            pltpu.VMEM((n_cols, n_cols), jnp.bfloat16),
            pltpu.VMEM((n_rows, 1), jnp.float32),
            pltpu.SemaphoreType.DMA((PARTS, 1 + len(targets))),
        ],
        compiler_params=pltpu.CompilerParams(vmem_limit_bytes=28 << 20),
    )(act, *((before,) if side else ()), rows, *targets)


def edges_of(decoder, encoder, row_ids, counts, activity):
    slot_count = row_ids.shape[1]
    owner = lax.axis_index("feat")

    picked_rows = decoder.at[row_ids[0]].get(mode="promise_in_bounds")
    owners = jnp.arange(counts.shape[1], dtype=jnp.int32)
    live_count = jnp.sum(jnp.where(owners == owner, counts[0], 0))
    live_slots = jnp.arange(slot_count, dtype=jnp.int32) < live_count
    source_rows = jnp.where(live_slots[:, None], picked_rows, jnp.zeros((), picked_rows.dtype))

    y0 = encoder
    y1 = send(y0, RING_Y)
    y2 = send(y1, RING_Y)
    y3 = send(y2, RING_Y)
    width = y0.shape[0]
    aa, dd = share(y0), share(y3)
    b1, b2 = send(y1, UP_X), send(y1, DOWN_X)
    c1, c2 = send(y2, UP_X), send(y2, DOWN_X)
    far = lax.dynamic_index_in_dim(aa, (lax.axis_index("prompt") // 4 + 2) % 4, 0, keepdims=False)
    f1 = send(far, RING_Y)
    f2 = send(f1, RING_Y)

    other = send(source_rows, OTHER_Y)
    own = jnp.concatenate([source_rows, other], axis=0)
    mine = lax.all_gather(own, "feat", axis=0, tiled=True, axis_index_groups=ROWS_Z)
    theirs = send(mine, CORE)

    act = activity.reshape(-1, 1)
    targets = [aa.reshape(4 * width, -1), y1, b1, b2, f1, y2, c1, c2, f2, dd.reshape(4 * width, -1)]
    part = product(act, mine, targets)
    return product(act, theirs, targets, part)[None]


def solution(mesh):
    in_specs = (
        P("feat", None),
        P(("feat", "prompt"), None),
        P("prompt", "feat"),
        P("prompt", None),
        P("prompt", None),
    )
    out_specs = P("prompt", None, "feat")
    return jax.shard_map(edges_of, mesh=mesh, in_specs=in_specs, out_specs=out_specs, check_vma=False)
```

```python
import functools

import jax
import jax.numpy as jnp
from jax import lax
from jax.experimental import pallas as pl
from jax.experimental.pallas import tpu as pltpu
from jax.sharding import PartitionSpec as P


AXES = ("prompt", "feat")


def routes(move):
    pairs = []
    for x in range(4):
        for y in range(8):
            for z in range(8):
                for core in range(2):
                    pairs.append((flat(x, y, z, core), flat(*move(x, y, z, core))))
    return pairs


def flat(x, y, z, core):
    prompt = (x % 4) * 4 + y % 4
    feat = ((y // 4) % 2 * 8 + z % 8) * 2 + core
    return prompt * 32 + feat


UP_X = routes(lambda x, y, z, c: (x + 1, y, z, c))
DOWN_X = routes(lambda x, y, z, c: (x - 1, y, z, c))
FAR_X = routes(lambda x, y, z, c: (x + 2, y, z, c))
RING_Y = routes(lambda x, y, z, c: (x, y // 4 * 4 + (y + (1 - 2 * c)) % 4, z, c))
OTHER_Y = routes(lambda x, y, z, c: (x, (y + 4) % 8, z, c))
CORE = routes(lambda x, y, z, c: (x, y, z, 1 - c))
ROWS_Z = [[(half * 8 + z) * 2 + core for z in range(8)] for half in range(2) for core in range(2)]

HOPS_X = (0, -1, 1, 2)
PARTS = 3


def send(value, pairs):
    return lax.ppermute(value, AXES, pairs)


def place():
    prompt, owner = lax.axis_index("prompt"), lax.axis_index("feat")
    chip = owner // 2
    return prompt // 4, prompt % 4, chip // 8, owner % 2


def product_kernel(n_sources, n_targets, first_block, last, *refs):
    act_ref, refs = refs[0], refs[1:]
    if last:
        (rows, before_ref), refs = refs[:2], refs[2:]
        sources = ()
    else:
        sources, refs = refs[:n_sources], refs[n_sources:]
    targets, refs = refs[:n_targets], refs[n_targets:]
    if last:
        out_ref, cols, acc, order, act, sem = refs
    else:
        out_ref, rows, cols, acc, order, act, sem = refs
    depth = rows.shape[1]
    width = depth // PARTS

    def copies(part):
        at_depth = pl.ds(pl.multiple_of(part * width, 128), width)
        found, i = [], 0
        for into, operands in ((rows, sources), (cols, targets)):
            at = 0
            for operand in operands:
                size = operand.shape[0]
                found.append(
                    pltpu.make_async_copy(
                        operand.at[:, at_depth], into.at[pl.ds(at, size), at_depth], sem.at[part, i]
                    )
                )
                at += size
                i += 1
        return found

    for part in range(PARTS):
        for copy in copies(part):
            copy.start()

    x, y, half, core = place()
    slots = act_ref.shape[0] // 32
    row_at = []
    for side in range(2):
        for flip in range(2):
            for z in range(8):
                feat = ((half ^ flip) * 8 + z) * 2 + (core ^ side)
                row_at.append(pl.multiple_of(feat * slots, slots))
    for g, at in enumerate(row_at):
        act[g * slots : (g + 1) * slots] = act_ref[pl.ds(at, slots)]
    block = out_ref.shape[1] // 16
    lane = lax.broadcasted_iota(jnp.int32, (block, out_ref.shape[1]), 1)
    line = lax.broadcasted_iota(jnp.int32, (block, out_ref.shape[1]), 0)
    for i in range(cols.shape[0] // block):
        step_y, hop = divmod(first_block + i, len(HOPS_X))
        origin = ((x + HOPS_X[hop]) & 3) * 4 + ((y - (1 - 2 * core) * step_y) & 3)
        order[i * block : (i + 1) * block] = jnp.where(lane == line + origin * block, 1.0, 0.0).astype(jnp.bfloat16)

    acc[...] = jnp.zeros_like(acc)

    @pl.loop(0, PARTS)
    def _(part):
        for copy in copies(part):
            copy.wait()
        at_depth = pl.ds(pl.multiple_of(part * width, 128), width)
        acc[...] += lax.dot_general(
            rows[:, at_depth], cols[:, at_depth], (((1,), (1,)), ((), ())), preferred_element_type=jnp.float32
        )

    edges = (acc[...] * act[...]).astype(jnp.bfloat16)
    placed = jnp.dot(edges, order[...], preferred_element_type=jnp.float32)
    if not last:
        out_ref[...] = placed.astype(jnp.bfloat16)
        return
    placed = (placed + before_ref[...].astype(jnp.float32)).astype(jnp.bfloat16)
    for g, at in enumerate(row_at):
        out_ref[pl.ds(at, slots), :] = placed[g * slots : (g + 1) * slots]


def product(act, first_block, sources, targets, rows=None, before=None):
    depth = targets[0].shape[1]
    n_rows = act.shape[0]
    n_cols, n_out = sum(t.shape[0] for t in targets), targets[0].shape[0] * 16
    whole, anywhere = pl.BlockSpec(memory_space=pltpu.VMEM), pl.BlockSpec(memory_space=pl.ANY)
    last = before is not None
    operands = (act, rows, before, *targets) if last else (act, *sources, *targets)
    edges_shape = jax.ShapeDtypeStruct((n_rows, n_out), jnp.bfloat16)
    rows_shape = jax.ShapeDtypeStruct((n_rows, depth), jnp.bfloat16)
    return pl.pallas_call(
        functools.partial(product_kernel, len(sources), len(targets), first_block, last),
        out_shape=edges_shape if last else (edges_shape, rows_shape),
        in_specs=[whole] * (3 if last else 1) + [anywhere] * (len(sources) + len(targets)),
        out_specs=whole if last else (whole, whole),
        scratch_shapes=[
            pltpu.VMEM((n_cols, depth), jnp.bfloat16),
            pltpu.VMEM((n_rows, n_cols), jnp.float32),
            pltpu.VMEM((n_cols, n_out), jnp.bfloat16),
            pltpu.VMEM((n_rows, 1), jnp.float32),
            pltpu.SemaphoreType.DMA((PARTS, len(sources) + len(targets))),
        ],
        compiler_params=pltpu.CompilerParams(vmem_limit_bytes=24 << 20),
    )(*operands)


def edges_of(decoder, encoder, row_ids, counts, activity):
    slot_count = row_ids.shape[1]
    owner = lax.axis_index("feat")

    picked_rows = decoder.at[row_ids[0]].get(mode="promise_in_bounds")
    owners = jnp.arange(counts.shape[1], dtype=jnp.int32)
    slots = jnp.arange(slot_count, dtype=jnp.int32)

    def live(of):
        return (slots < jnp.sum(jnp.where(owners == of, counts[0], 0)))[:, None]

    zero = jnp.zeros((), picked_rows.dtype)
    live_here, live_there = live(owner), live(owner ^ 16)
    source_rows = jnp.where(live_here, picked_rows, zero)

    y0 = encoder
    y1 = send(y0, RING_Y)
    y2 = send(y1, RING_Y)
    y3 = send(y2, RING_Y)
    a1, a2, a3 = send(y0, UP_X), send(y0, DOWN_X), send(y0, FAR_X)
    b1, b2 = send(y1, UP_X), send(y1, DOWN_X)
    c1, c2 = send(y2, UP_X), send(y2, DOWN_X)
    d1, d2, d3 = send(y3, UP_X), send(y3, DOWN_X), send(y3, FAR_X)
    f1 = send(a3, RING_Y)
    f2 = send(f1, RING_Y)

    mine = lax.all_gather(source_rows, "feat", axis=0, tiled=True, axis_index_groups=ROWS_Z)
    sent = send(picked_rows, OTHER_Y)
    other = jnp.where(live_there, sent, zero)
    mine_too = lax.all_gather(other, "feat", axis=0, tiled=True, axis_index_groups=ROWS_Z)
    sources = [mine, mine_too, send(mine, CORE), send(mine_too, CORE)]

    act = activity.reshape(-1, 1)
    part, rows = product(act, 0, sources, [y0, a1, a2, a3, y1, b1, b2, f1, y2, c1, c2, f2])
    edges = product(act, 12, [], [y3, d1, d2, d3], rows, part)
    return edges[None]


def solution(mesh):
    in_specs = (
        P("feat", None),
        P(("feat", "prompt"), None),
        P("prompt", "feat"),
        P("prompt", None),
        P("prompt", None),
    )
    out_specs = P("prompt", None, "feat")
    return jax.shard_map(edges_of, mesh=mesh, in_specs=in_specs, out_specs=out_specs, check_vma=False)
```

```python
import functools

import jax
import jax.numpy as jnp
from jax import lax
from jax.experimental import pallas as pl
from jax.experimental.pallas import tpu as pltpu
from jax.sharding import PartitionSpec as P


AXES = ("prompt", "feat")


def routes(move):
    pairs = []
    for x in range(4):
        for y in range(8):
            for z in range(8):
                for core in range(2):
                    pairs.append((flat(x, y, z, core), flat(*move(x, y, z, core))))
    return pairs


def flat(x, y, z, core):
    prompt = (x % 4) * 4 + y % 4
    feat = ((y // 4) % 2 * 8 + z % 8) * 2 + core
    return prompt * 32 + feat


UP_X = routes(lambda x, y, z, c: (x + 1, y, z, c))
DOWN_X = routes(lambda x, y, z, c: (x - 1, y, z, c))
RING_Y = routes(lambda x, y, z, c: (x, y // 4 * 4 + (y + (1 - 2 * c)) % 4, z, c))
OTHER_Y = routes(lambda x, y, z, c: (x, (y + 4) % 8, z, c))
UP_Z = routes(lambda x, y, z, c: (x, y, z + 1, c))
DOWN_Z = routes(lambda x, y, z, c: (x, y, z - 1, c))
CORE = routes(lambda x, y, z, c: (x, y, z, 1 - c))
ROWS_X = [[x * 4 + y for x in range(4)] for y in range(4)]

HOPS_Z = (0, -1, 1, -2, 2, -3, 3, -4)
ALL_X = tuple((None, x) for x in range(4))
BLOCKS = (
    *((0, *at) for at in ALL_X),
    *((step, hop, None) for step in (1, 2) for hop in (0, -1, 1, 2)),
    *((3, *at) for at in ALL_X),
)
PARTS = 3


def send(value, pairs):
    return lax.ppermute(value, AXES, pairs)


def share(value):
    copies = jnp.broadcast_to(value[None], (4,) + value.shape)
    return lax.all_to_all(copies, "prompt", 0, 0, axis_index_groups=ROWS_X, tiled=True)


def stack_kernel(*refs):
    operands, (out_ref, held, sem) = refs[:-3], refs[-3:]
    inward, outward, at = [], [], 0
    for i, operand in enumerate(operands):
        lines = pl.ds(at, operand.shape[0])
        inward.append(pltpu.make_async_copy(operand, held.at[lines], sem.at[0, i]))
        outward.append(pltpu.make_async_copy(held.at[lines], out_ref.at[lines], sem.at[1, i]))
        at += operand.shape[0]
    for copy in inward:
        copy.start()
    for copy, onward in zip(inward, outward):
        copy.wait()
        onward.start()
    for copy in outward:
        copy.wait()


def stack(*pieces):
    shape = (sum(piece.shape[0] for piece in pieces), pieces[0].shape[1])
    return pl.pallas_call(
        stack_kernel,
        out_shape=jax.ShapeDtypeStruct(shape, pieces[0].dtype),
        in_specs=[pl.BlockSpec(memory_space=pl.ANY)] * len(pieces),
        out_specs=pl.BlockSpec(memory_space=pl.ANY),
        scratch_shapes=[pltpu.VMEM(shape, pieces[0].dtype), pltpu.SemaphoreType.DMA((2, len(pieces)))],
    )(*pieces)


def place():
    prompt, owner = lax.axis_index("prompt"), lax.axis_index("feat")
    chip = owner // 2
    return prompt // 4, prompt % 4, chip // 8, chip % 8, owner % 2


def product_kernel(n_sources, act_ref, *refs):
    operands, (out_ref, rows, cols, acc, order, natural, act, sem) = refs[:-8], refs[-8:]
    sources, targets = operands[:n_sources], operands[n_sources:]
    width = rows.shape[1] // PARTS

    def copies(part):
        at_depth = pl.ds(pl.multiple_of(part * width, 128), width)
        found, i = [], 0
        for into, pieces in ((rows, sources), (cols, targets)):
            at = 0
            for piece in pieces:
                size = piece.shape[0]
                found.append(
                    pltpu.make_async_copy(
                        piece.at[:, at_depth], into.at[pl.ds(at, size), at_depth], sem.at[part, i]
                    )
                )
                at += size
                i += 1
        return found

    for part in range(PARTS):
        for copy in copies(part):
            copy.start()

    x, y, half, z, core = place()
    slots = act_ref.shape[1] // 32
    row_at = []
    for side in range(2):
        for hop in HOPS_Z:
            for flip in range(2):
                feat = ((half ^ flip) * 8 + ((z + hop) & 7)) * 2 + (core ^ side)
                row_at.append(pl.multiple_of(feat * slots, slots))
    natural[...] = jnp.broadcast_to(act_ref[...], (128, act_ref.shape[1])).T
    for g, at in enumerate(row_at):
        act[g * slots : (g + 1) * slots] = natural[pl.ds(at, slots), :1]
    block = out_ref.shape[1] // 16
    lane = lax.broadcasted_iota(jnp.int32, (block, out_ref.shape[1]), 1)
    line = lax.broadcasted_iota(jnp.int32, (block, out_ref.shape[1]), 0)
    for i, (step_y, hop, x_there) in enumerate(BLOCKS):
        x_from = x_there if hop is None else (x + hop) & 3
        origin = x_from * 4 + ((y - (1 - 2 * core) * step_y) & 3)
        order[i * block : (i + 1) * block] = jnp.where(lane == line + origin * block, 1.0, 0.0).astype(jnp.bfloat16)

    acc[...] = jnp.zeros_like(acc)

    @pl.loop(0, PARTS)
    def _(part):
        for copy in copies(part):
            copy.wait()
        at_depth = pl.ds(pl.multiple_of(part * width, 128), width)
        acc[...] += lax.dot_general(
            rows[:, at_depth], cols[:, at_depth], (((1,), (1,)), ((), ())), preferred_element_type=jnp.float32
        )

    edges = (acc[...] * act[...]).astype(jnp.bfloat16)
    placed = jnp.dot(edges, order[...], preferred_element_type=jnp.float32).astype(jnp.bfloat16)
    for g, at in enumerate(row_at):
        out_ref[pl.ds(at, slots), :] = placed[g * slots : (g + 1) * slots]


def product(act, sources, targets):
    depth = targets[0].shape[1]
    n_rows, n_cols = act.shape[1], sum(t.shape[0] for t in targets)
    whole, anywhere = pl.BlockSpec(memory_space=pltpu.VMEM), pl.BlockSpec(memory_space=pltpu.HBM)
    return pl.pallas_call(
        functools.partial(product_kernel, len(sources)),
        out_shape=jax.ShapeDtypeStruct((n_rows, n_cols), jnp.bfloat16),
        in_specs=[whole] + [anywhere] * (len(sources) + len(targets)),
        out_specs=whole,
        scratch_shapes=[
            pltpu.VMEM((n_rows, depth), jnp.bfloat16),
            pltpu.VMEM((n_cols, depth), jnp.bfloat16),
            pltpu.VMEM((n_rows, n_cols), jnp.float32),
            pltpu.VMEM((n_cols, n_cols), jnp.bfloat16),
            pltpu.VMEM((n_rows, 128), jnp.float32),
            pltpu.VMEM((n_rows, 1), jnp.float32),
            pltpu.SemaphoreType.DMA((PARTS, len(sources) + len(targets))),
        ],
        compiler_params=pltpu.CompilerParams(vmem_limit_bytes=28 << 20),
        name="product",
    )(act, *sources, *targets)


def edges_of(decoder, encoder, row_ids, counts, activity):
    slot_count = row_ids.shape[1]
    owner = lax.axis_index("feat")

    picked_rows = decoder.at[row_ids[0]].get(mode="promise_in_bounds")
    owners = jnp.arange(counts.shape[1], dtype=jnp.int32)
    live_count = jnp.sum(jnp.where(owners == owner, counts[0], 0))
    live_slots = jnp.arange(slot_count, dtype=jnp.int32) < live_count
    source_rows = jnp.where(live_slots[:, None], picked_rows, jnp.zeros((), picked_rows.dtype))

    y0 = encoder
    y1 = send(y0, RING_Y)
    y2 = send(y1, RING_Y)
    y3 = send(y2, RING_Y)
    width = y0.shape[0]
    aa, dd = share(y0), share(y3)
    b1, b2 = send(y1, UP_X), send(y1, DOWN_X)
    c1, c2 = send(y2, UP_X), send(y2, DOWN_X)
    far = lax.dynamic_index_in_dim(aa, (lax.axis_index("prompt") // 4 + 2) % 4, 0, keepdims=False)
    f1 = send(far, RING_Y)
    f2 = send(f1, RING_Y)

    other = send(source_rows, OTHER_Y)
    own = jnp.concatenate([source_rows, other], axis=0)
    u1, w1 = send(own, UP_Z), send(own, DOWN_Z)
    u2, w2 = send(u1, UP_Z), send(w1, DOWN_Z)
    u3, w3 = send(u2, UP_Z), send(w2, DOWN_Z)
    u4 = send(u3, UP_Z)
    near = stack(own, u1, w1, u2, w2)
    away = stack(u3, w3, u4)
    sources = [own, u1, w1, u2, w2, u3, w3, u4, send(near, CORE), send(away, CORE)]

    targets = [aa.reshape(4 * width, -1), y1, b1, b2, f1, y2, c1, c2, f2, dd.reshape(4 * width, -1)]
    return product(activity, sources, targets)[None]


def solution(mesh):
    in_specs = (
        P("feat", None),
        P(("feat", "prompt"), None),
        P("prompt", "feat"),
        P("prompt", None),
        P("prompt", None),
    )
    out_specs = P("prompt", None, "feat")
    return jax.shard_map(edges_of, mesh=mesh, in_specs=in_specs, out_specs=out_specs, check_vma=False)
```
